32 devices in a mesh: seq: 8 (over y, x, core), head: 4 (over z).
Axes of the slice: x: 2, y: 2, z: 4, core: 2. Of those that a mesh axis runs over, the one named last changes fastest.
Arguments:
- lengths: int32 [16], replicated, may hold values from 1 to 1024, 2048 in all
- query: bfloat16 [2048, 8192], P('seq', 'head'), may hold values from -4.5 to 4.5
- keys: bfloat16 [2048, 1024], P('seq', 'head'), may hold values from -4.5 to 4.5
- values: bfloat16 [2048, 1024], P('seq', 'head'), may hold values from -6 to 6
- attention_grad: bfloat16 [2048, 8192], P('seq', 'head'), may hold values from -6 to 6
Outputs:
- attention_out: bfloat16 [2048, 8192], P('seq', 'head')
- query_grad: bfloat16 [2048, 8192], P('seq', 'head')
- key_grad: bfloat16 [2048, 1024], P('seq', 'head')
- value_grad: bfloat16 [2048, 1024], P('seq', 'head')
The draws below stay inside these ranges and needn't reach their ends.
Inputs may be any that keep to these rules, and one draw needn't show every extreme that they name: The lengths sum to 2048 and the longest is exactly 1024.
All inputs are finite; a program needn't handle non-finite values.
Results may differ from the reference program's by a relative error of at most 0.023.
Values may be sent and summed in bfloat16 or wider, within the bound.
A program may use at most 128 MiB of HBM per device.

```python
import math
import jax
import jax.numpy as jnp
import numpy as np
from jax import lax

ATT_HEADS = 64
KV_HEADS = 8
ATT_DIM = 128
DOCS = 16
PACKED_TOKENS = 2048
DOC_MOST = 1024


def query_key_pair(key):
    width_query = ATT_HEADS * ATT_DIM
    width_key = KV_HEADS * ATT_DIM
    query = jnp.clip(jax.random.normal(jax.random.fold_in(key, 11), (PACKED_TOKENS, width_query)), -4.0, 4.0)
    keyed = jnp.clip(jax.random.normal(jax.random.fold_in(key, 12), (PACKED_TOKENS, width_key)), -4.0, 4.0)
    return (query, keyed)


def draw_query(key, part):
    return query_key_pair(key)[0].astype(jnp.bfloat16)


def draw_keys(key, part):
    return query_key_pair(key)[1].astype(jnp.bfloat16)


def levels(own_key, shape, pieces, low, top_value):
    def one(axis_at, parts):
        steps = jax.random.uniform(jax.random.fold_in(jax.random.fold_in(own_key, 6), axis_at), (parts,), jnp.float32, low / len(pieces), top_value / len(pieces))
        return jnp.repeat(jnp.exp(steps), shape[axis_at] // parts).reshape((-1,) + (1,) * (len(shape) - axis_at - 1))

    level = one(*pieces[0])
    for cut in pieces[1:]:
        level = level * one(*cut)
    return level


def profile(count, total, most, skew):
    loads = [(1 << 20) // math.isqrt(rank ** skew) + 1 for rank in range(2, count + 1)]
    surplus, holding = total - most - (count - 1), [1] * (count - 1)
    while surplus > 0:
        candidates = [i for i in range(count - 1) if holding[i] < most]
        whole, left = sum([loads[i] for i in candidates]), surplus
        for i in candidates:
            more = min(most - holding[i], max(1, left * loads[i] // whole), surplus)
            holding[i] = holding[i] + more
            surplus = surplus - more
    return np.array([most] + holding)


def uneven(own_key, amount, total, most, lean):
    if amount == 2:
        one = jax.random.randint(own_key, (), max(1, total - most), min(most, total - 1) + 1)
        return jnp.stack([one, total - one])
    sizes = jnp.asarray(profile(amount, total, most, lean), jnp.int32)
    pairs = (amount - 1) // 2
    donor, sink = sizes[1:1 + 2 * pairs:2], sizes[2:2 + 2 * pairs:2]
    margin = jnp.minimum(donor - 1, most - sink)
    passed = jax.random.randint(jax.random.fold_in(own_key, 1), (pairs,), 0, 1 << 20) % (margin + 1)
    sizes = sizes.at[1:1 + 2 * pairs:2].set(donor - passed).at[2:2 + 2 * pairs:2].set(sink + passed)
    return sizes[jax.random.permutation(jax.random.fold_in(own_key, 2), amount)]


def bell_draw(stream_key, dims, deviation, most, cuts=(), kind=jnp.bfloat16):
    entries = jax.random.normal(stream_key, dims, jnp.float32) * deviation
    if len(cuts) > 0:
        entries = levels(stream_key, dims, cuts, -0.22, 0.18) * entries
    return jnp.clip(entries, min=-most, max=most).astype(kind)


def setup_inputs(seed: int = 0) -> dict:
    seeds = jax.random.split(jax.random.key(seed), 6)
    lengths = uneven(seeds[0], DOCS, PACKED_TOKENS, DOC_MOST, 2).astype(jnp.int32)
    query = draw_query(jax.random.fold_in(seeds[5], 71), 0)
    keys = draw_keys(jax.random.fold_in(seeds[5], 71), 0)
    values = bell_draw(seeds[3], (PACKED_TOKENS, KV_HEADS * ATT_DIM), 1.0, 6.0, ((0, 8), (1, 4)))
    attention_grad = bell_draw(seeds[4], (PACKED_TOKENS, ATT_HEADS * ATT_DIM), 1.0, 6.0, ((0, 8), (1, 4)))
    return {"lengths": lengths, "query": query, "keys": keys, "values": values, "attention_grad": attention_grad}


masked_score = -1.0e30


def segment_of(position, ends):
    return jnp.sum((ends[None, :] <= position[:, None]).astype(jnp.int32), axis=1)


def reference(lengths, query, keys, values, attention_grad):
    total = query.shape[0]
    share = ATT_HEADS // KV_HEADS
    position = jnp.arange(total, dtype=jnp.int32)
    ends = jnp.cumsum(lengths).astype(jnp.int32)
    segment = segment_of(position, ends)
    allowed = (segment[:, None] == segment[None, :]) & (position[:, None] >= position[None, :])
    scale = ATT_DIM ** -0.5
    group_of = jnp.arange(ATT_HEADS, dtype=jnp.int32) // share

    def split_heads(array, count):
        return array.reshape(total, count, ATT_DIM).transpose(1, 0, 2)

    def one_head(operands):
        head_q, head_k, head_v, head_g = operands
        score = jnp.dot(head_q, head_k.T, preferred_element_type=jnp.float32) * scale
        score = jnp.where(allowed, score, masked_score)
        top = jnp.max(score, axis=1, keepdims=True)
        mass = jnp.sum(jnp.where(allowed, jnp.exp(score - top), 0.0), axis=1, keepdims=True)
        log_total = top + jnp.log(mass)
        prob = jnp.where(allowed, jnp.exp(score - log_total), 0.0)
        prob_b = prob.astype(jnp.bfloat16)
        attn_out = jnp.dot(prob_b, head_v, preferred_element_type=jnp.float32)
        delta = jnp.sum(head_g.astype(jnp.float32) * attn_out, axis=1, keepdims=True)
        dprob = jnp.dot(head_g, head_v.T, preferred_element_type=jnp.float32)
        dscore = (prob * (dprob - delta) * scale).astype(jnp.bfloat16)
        grad_q = jnp.dot(dscore, head_k, preferred_element_type=jnp.float32).astype(jnp.bfloat16)
        grad_k = jnp.dot(dscore.T, head_q, preferred_element_type=jnp.float32)
        grad_v = jnp.dot(prob_b.T, head_g, preferred_element_type=jnp.float32)
        return attn_out.astype(jnp.bfloat16), grad_q, grad_k, grad_v

    key_heads = split_heads(keys, KV_HEADS)[group_of]
    value_heads = split_heads(values, KV_HEADS)[group_of]
    outputs, grad_q, grad_k, grad_v = lax.map(one_head, (split_heads(query, ATT_HEADS), key_heads, value_heads, split_heads(attention_grad, ATT_HEADS)))
    grad_k = jnp.sum(grad_k.reshape(KV_HEADS, share, total, ATT_DIM), axis=1).astype(jnp.bfloat16)
    grad_v = jnp.sum(grad_v.reshape(KV_HEADS, share, total, ATT_DIM), axis=1).astype(jnp.bfloat16)

    def merge_heads(array):
        return array.transpose(1, 0, 2).reshape(total, -1)

    return (merge_heads(outputs), merge_heads(grad_q), merge_heads(grad_k), merge_heads(grad_v))
```

```python
import functools

import jax
import jax.numpy as jnp
from jax import lax
from jax.experimental import pallas as pl
from jax.experimental.pallas import tpu as pltpu
from jax.sharding import PartitionSpec as P

ATT_DIM = 128
LOG2E = 1.4426950408889634
MASKED = -1.0e30
MESH = pl.DeviceIdType.MESH

F32 = jnp.float32
BF16 = jnp.bfloat16
NT = (((1,), (1,)), ((), ()))
NN = (((1,), (0,)), ((), ()))
DK, DV = 0, 1
ONES = 16
FOLD = 32


def interleave(*runs):
    runs = list(runs)
    while runs:
        runs = [run for run in runs if next(run, True) is None]


def kernel(
    n, span, kv_count, share,
    lengths, query_hbm, keys, values, grad_hbm,
    out, query_grad, key_grad, value_grad,
    query, grad, kv, key_t, value_t, query_t, grad_t, delta, top, bias, score_a, score_b, score_c, prob,
    acc, sent, mix, got,
    load, gather_send, gather_recv, back_send, mix_recv, back_recv,
):
    rows = query.shape[0]
    scale = ATT_DIM ** -0.5
    me = lax.axis_index("seq")
    odd = lax.rem(me, 2)
    pair = me + 1 - 2 * odd
    far = span // 2
    score = (score_a, score_b, score_c)

    def load_kv(g, which):
        columns = pl.ds(pl.multiple_of(g * ATT_DIM, ATT_DIM), ATT_DIM)
        source = (keys, values)[which]
        return pltpu.make_async_copy(
            source.at[:, columns], kv.at[g, 0, which], load.at[2 + 2 * g + which]
        )

    def start_load(g, _):
        load_kv(g, 0).start()
        load_kv(g, 1).start()
        return 0

    lax.fori_loop(0, kv_count, start_load, 0)
    load_query = pltpu.make_async_copy(query_hbm, query, load.at[0])
    load_grad = pltpu.make_async_copy(grad_hbm, grad, load.at[1])
    load_query.start()
    load_grad.start()

    def signal(barrier, target):
        pl.semaphore_signal(barrier, inc=1, device_id={"seq": target}, device_id_type=MESH)

    barrier = pltpu.get_barrier_semaphore()
    signal(barrier, pair)
    for j in range(1, far + 1):
        @pl.when(me + 2 * j < n)
        def _():
            signal(barrier, me + 2 * j)

        @pl.when(me - 2 * j >= 0)
        def _():
            signal(barrier, me - 2 * j)

    def clear(g, _):
        for k in range(1, span):
            @pl.when(me - k < 0)
            def _():
                kv[g, k] = jnp.zeros((2, rows, ATT_DIM), BF16)
        return 0

    lax.fori_loop(0, kv_count, clear, 0)
    q_lane = lax.broadcasted_iota(jnp.int32, (1, rows), 1)
    position = q_lane + me * rows
    start = jnp.zeros((1, rows), jnp.int32)
    end = 0
    for i in range(lengths.shape[0]):
        end = end + lengths[i]
        start = jnp.where(position >= end, end, start)

    k_row = lax.broadcasted_iota(jnp.int32, (rows, rows), 0)
    for k in range(span):
        allow = k_row >= start - (me - k) * rows
        if k == 0:
            allow = allow & (k_row <= q_lane)
        bias[k * rows:(k + 1) * rows, :] = jnp.where(allow, 0.0, MASKED)
    value_t[ATT_DIM:, :] = jnp.ones((ONES, value_t.shape[1]), BF16)
    pl.semaphore_wait(
        barrier, 1 + jnp.minimum(me // 2, far) + jnp.minimum((n - 1 - me) // 2, far)
    )

    def remote(source, target, send_sem, recv_sem, device):
        return pltpu.make_async_remote_copy(
            src_ref=source, dst_ref=target, send_sem=send_sem, recv_sem=recv_sem,
            device_id={"seq": device}, device_id_type=MESH,
        )

    def gather(g, j):
        return remote(
            kv.at[g, 0], kv.at[g, 2 * j], gather_send.at[g, 2 * j],
            gather_recv.at[g, 2 * j], me + 2 * j,
        )

    def hand_on(g, j, slot):
        return remote(
            kv.at[g, 2 * j], kv.at[g, slot], gather_send.at[g, slot],
            gather_recv.at[g, slot], pair,
        )

    def each_hand_on(first, last, act):
        for j in range(first, last + 1):
            if j >= 1:
                @pl.when((odd == 1) & (me - 2 * j >= 0))
                def _():
                    act(j, 2 * j - 1)
            if j < far:
                @pl.when((odd == 0) & (me - 2 * j >= 0))
                def _():
                    act(j, 2 * j + 1)

    def begin(g):
        load_kv(g, 0).wait()
        load_kv(g, 1).wait()
        for j in range(1, far + 1):
            @pl.when(me + 2 * j < n)
            def _():
                gather(g, j).start()
        each_hand_on(0, 0, lambda j, slot: hand_on(g, j, slot).start())

    begin(0)

    def pass_on(g):
        for j in range(1, far + 1):
            @pl.when(me - 2 * j >= 0)
            def _():
                gather(g, j).wait_recv()
            each_hand_on(j, j, lambda j, slot: hand_on(g, j, slot).start())

    def partial(g, which, k):
        part = acc[g, which, :, k * rows:(k + 1) * rows]
        return part * (1.0 / scale) if which == DV else part

    def to_pair(g, which, k, j):
        return remote(
            sent.at[g, which, k], mix.at[g, which, j], back_send.at[g, which, k],
            mix_recv.at[g, which, j], pair,
        )

    def back(g, which, j):
        return remote(
            sent.at[g, which, 2 * j], got.at[g, which, j], back_send.at[g, which, 2 * j],
            back_recv.at[g, which, j], me - 2 * j,
        )

    def each_to_pair(act):
        for k in range(1, span, 2):
            @pl.when((odd == 1) & (me - k >= 0))
            def _():
                act(k, (k - 1) // 2)

            @pl.when((odd == 0) & (me - k >= 0))
            def _():
                act(k, (k + 1) // 2)

    def share_partial(g, which):
        def act(k, j):
            sent[g, which, k] = partial(g, which, k).astype(BF16)
            to_pair(g, which, k, j).start()

        each_to_pair(act)

    def wait_mix(g, which, j):
        to_pair(g, which, 1, j).wait_recv()

    def combine(g, which):
        for j in range(far, 0, -1):
            def give(mixed):
                part = partial(g, which, 2 * j)
                if mixed:
                    wait_mix(g, which, j)
                    part = part + mix[g, which, j].astype(F32)
                sent[g, which, 2 * j] = part.astype(BF16)
                back(g, which, j).start()

            if j < far:
                @pl.when(me - 2 * j >= 0)
                def _():
                    give(True)
            else:
                @pl.when((me - 2 * j >= 0) & (odd == 1))
                def _():
                    give(True)

                @pl.when((me - 2 * j >= 0) & (odd == 0))
                def _():
                    give(False)

    load_query.wait()
    load_grad.wait()
    pass_on(0)

    def group(g, _):
        for k in range(1, span, 2):
            @pl.when(me - k >= 0)
            def _():
                hand_on(g, 0, k).wait_recv()
        for k in range(span):
            key_t[:, k * rows:(k + 1) * rows] = kv[g, k, 0].T
            value_t[:ATT_DIM, k * rows:(k + 1) * rows] = kv[g, k, 1].T
        if kv_count > 1:
            @pl.when(g + 1 < kv_count)
            def _():
                begin(g + 1)

        def columns(h):
            return pl.ds(pl.multiple_of((g * share + h) * ATT_DIM, ATT_DIM), ATT_DIM)

        def at(k):
            return slice(k * rows, (k + 1) * rows)

        def add(which, h, k, a, b):
            part = lax.dot_general(a, b, NT, preferred_element_type=F32)
            if h:
                part = acc[g, which, :, at(k)] + part
            acc[g, which, :, at(k)] = part

        def scores(h, slot):
            q_t = query[:, columns(h)].T
            query_t[h] = q_t
            most = jnp.full((FOLD, rows), MASKED, F32)
            for k in range(span):
                s = lax.dot_general(kv[g, k, 0], q_t, NN, preferred_element_type=F32)
                s = s + bias[at(k), :]
                score[slot][at(k), :] = s
                for r in range(0, rows, FOLD):
                    most = jnp.maximum(most, s[r:r + FOLD])
                yield
            top[slot] = jnp.max(most, axis=0, keepdims=True)

        def softmax(h, slot):
            peak = top[slot]
            out_t = jnp.zeros((ATT_DIM + ONES, rows), F32)
            for k in range(span):
                p = jnp.exp2((score[slot][at(k), :] - peak) * (scale * LOG2E))
                p = p.astype(BF16)
                prob[h, at(k), :] = p
                out_t = out_t + lax.dot_general(
                    value_t[:, at(k)], p, NN, preferred_element_type=F32
                )
                yield
            inverse = 1.0 / out_t[ATT_DIM:ATT_DIM + 1]
            out_t = out_t[:ATT_DIM] * inverse
            out[:, columns(h)] = out_t.astype(BF16).T
            factor = inverse * scale
            g_t = grad[:, columns(h)].T.astype(F32) * factor
            delta[h] = jnp.sum(g_t * out_t, axis=0, keepdims=True)
            grad_t[h] = g_t.astype(BF16)

        def value_sums(h):
            for k in range(span):
                add(DV, h, k, grad_t[h], prob[h, at(k), :])
                yield

        def slopes(h, slot):
            for k in range(span):
                score[slot][at(k), :] = lax.dot_general(
                    kv[g, k, 1], grad_t[h], NN, preferred_element_type=F32
                )
                yield

        def key_sums(h, slot):
            low = delta[h]
            dq = jnp.zeros((ATT_DIM, rows), F32)
            for k in range(span):
                ds = prob[h, at(k), :] * (score[slot][at(k), :] - low).astype(BF16)
                dq = dq + lax.dot_general(key_t[:, at(k)], ds, NN, preferred_element_type=F32)
                add(DK, h, k, query_t[h], ds)
                yield
            query_grad[:, columns(h)] = dq.astype(BF16).T

        def ahead(h):
            if h < share:
                return scores(h, h % 3)
            return slopes(h - share, h % 3)

        interleave(ahead(0), ahead(1))
        for h in range(share):
            runs = [softmax(h, h % 3), ahead(h + 2)]
            interleave(*runs)
        if kv_count > 1:
            @pl.when(g >= 1)
            def _():
                combine(g - 1, DK)
        for h in range(share):
            if h == share // 2:
                if kv_count > 1:
                    @pl.when(g + 1 < kv_count)
                    def _():
                        pass_on(g + 1)
            runs = [key_sums(h, (h + share) % 3)]
            if h + 2 < share:
                runs.append(slopes(h + 2, (h + 2 + share) % 3))
            runs.append(value_sums(h))
            interleave(*runs)
        share_partial(g, DV)
        combine(g, DV)
        share_partial(g, DK)
        return 0

    lax.fori_loop(0, kv_count, group, 0)
    combine(kv_count - 1, DK)

    def finish(g, _):
        columns = pl.ds(pl.multiple_of(g * ATT_DIM, ATT_DIM), ATT_DIM)
        for which, target in ((DV, value_grad), (DK, key_grad)):
            unit = scale if which == DV else 1.0

            @pl.when(odd == 0)
            def _():
                wait_mix(g, which, 0)
                acc[g, which, :, 0:rows] += mix[g, which, 0].astype(F32) * unit

            for j in range(1, far + 1):
                @pl.when(me + 2 * j < n)
                def _():
                    back(g, which, j).wait_recv()
                    acc[g, which, :, 0:rows] += got[g, which, j].astype(F32) * unit
            target[:, columns] = partial(g, which, 0).T.astype(BF16)
            for j in range(1, far + 1):
                @pl.when(me - 2 * j >= 0)
                def _():
                    back(g, which, j).wait_send()
            each_to_pair(lambda k, j: to_pair(g, which, k, j).wait_send())
        for j in range(1, far + 1):
            @pl.when(me + 2 * j < n)
            def _():
                gather(g, j).wait_send()
        each_hand_on(0, far, lambda j, slot: hand_on(g, j, slot).wait_send())
        return 0

    lax.fori_loop(0, kv_count, finish, 0)


def deliver(*refs):
    sources, targets, buffers = refs[:4], refs[4:8], refs[8:12]
    first, second = refs[12], refs[13]
    parts = []
    for i in range(4):
        rows = sources[i].shape[0]
        cuts = 4 if i < 2 else 1
        for c in range(cuts):
            at = pl.ds(c * rows // cuts, rows // cuts)
            m = len(parts)
            parts.append((
                pltpu.make_async_copy(sources[i].at[at], buffers[i].at[at], first.at[m]),
                pltpu.make_async_copy(buffers[i].at[at], targets[i].at[at], second.at[m]),
            ))
    for fetch, _ in parts:
        fetch.start()
    for fetch, write in parts:
        fetch.wait()
        write.start()
    for _, write in parts:
        write.wait()


def on_device(lengths, query, keys, values, attention_grad):
    n = lax.axis_size("seq")
    rows = query.shape[0]
    kv_count = keys.shape[1] // ATT_DIM
    share = query.shape[1] // keys.shape[1]
    span = n // 2 + 1
    whole = pl.BlockSpec(memory_space=pltpu.VMEM)
    hbm = pl.BlockSpec(memory_space=pltpu.HBM)
    keyed = span * rows
    turned = (ATT_DIM, rows)
    results = pl.pallas_call(
        functools.partial(kernel, n, span, kv_count, share),
        out_shape=[
            jax.ShapeDtypeStruct(a.shape, BF16) for a in (query, query, keys, values)
        ],
        in_specs=[pl.BlockSpec(memory_space=pltpu.SMEM)]
        + [pl.BlockSpec(memory_space=pl.ANY)] * 4,
        out_specs=[whole] * 4,
        scratch_shapes=[
            pltpu.VMEM(query.shape, BF16),
            pltpu.VMEM(query.shape, BF16),
            pltpu.VMEM((kv_count, span, 2, rows, ATT_DIM), BF16),
            pltpu.VMEM((ATT_DIM, keyed), BF16),
            pltpu.VMEM((ATT_DIM + ONES, keyed), BF16),
            pltpu.VMEM((share,) + turned, BF16),
            pltpu.VMEM((share,) + turned, BF16),
            pltpu.VMEM((share, 1, rows), F32),
            pltpu.VMEM((3, 1, rows), F32),
            pltpu.VMEM((keyed, rows), F32),
            pltpu.VMEM((keyed, rows), F32),
            pltpu.VMEM((keyed, rows), F32),
            pltpu.VMEM((keyed, rows), F32),
            pltpu.VMEM((share, keyed, rows), BF16),
            pltpu.VMEM((kv_count, 2, ATT_DIM, keyed), F32),
            pltpu.VMEM((kv_count, 2, span) + turned, BF16),
            pltpu.VMEM((kv_count, 2, span // 2 + 1) + turned, BF16),
            pltpu.VMEM((kv_count, 2, span // 2 + 1) + turned, BF16),
            pltpu.SemaphoreType.DMA((2 + 2 * kv_count,)),
            pltpu.SemaphoreType.DMA((kv_count, span)),
            pltpu.SemaphoreType.DMA((kv_count, span)),
            pltpu.SemaphoreType.DMA((kv_count, 2, span)),
            pltpu.SemaphoreType.DMA((kv_count, 2, span // 2 + 1)),
            pltpu.SemaphoreType.DMA((kv_count, 2, span // 2 + 1)),
        ],
        compiler_params=pltpu.CompilerParams(
            collective_id=0, has_side_effects=True, vmem_limit_bytes=60 << 20
        ),
    )(lengths, query, keys, values, attention_grad)
    return pl.pallas_call(
        deliver,
        out_shape=[jax.ShapeDtypeStruct(a.shape, BF16) for a in results],
        in_specs=[hbm] * 4,
        out_specs=[hbm] * 4,
        scratch_shapes=[pltpu.VMEM(a.shape, BF16) for a in results]
        + [pltpu.SemaphoreType.DMA((10,)), pltpu.SemaphoreType.DMA((10,))],
    )(*results)


def solution(mesh):
    in_specs = (P(), P("seq", "head"), P("seq", "head"), P("seq", "head"), P("seq", "head"))
    out_specs = (P("seq", "head"), P("seq", "head"), P("seq", "head"), P("seq", "head"))
    return jax.shard_map(
        on_device, mesh=mesh, in_specs=in_specs, out_specs=out_specs, check_vma=False
    )
```

```python
import functools

import jax
import jax.numpy as jnp
from jax import lax
from jax.experimental import pallas as pl
from jax.experimental.pallas import tpu as pltpu
from jax.sharding import PartitionSpec as P

ATT_DIM = 128
LOG2E = 1.4426950408889634
MASKED = -1.0e30
MESH = pl.DeviceIdType.MESH

F32 = jnp.float32
BF16 = jnp.bfloat16
NT = (((1,), (1,)), ((), ()))
NN = (((1,), (0,)), ((), ()))
DK, DV = 0, 1
ONES = 16
FOLD = 32


def interleave(*runs):
    runs = list(runs)
    while runs:
        runs = [run for run in runs if next(run, True) is None]


def kernel(
    n, span, kv_count, share,
    lengths, query_hbm, keys, values, grad_hbm,
    out_hbm, query_grad_hbm, key_grad, value_grad,
    query, grad, out, query_grad, kv, key_t, value_t, query_t, cot_t, grad_t, delta, factors,
    top, near_top, near_score, near_slope, bias, score_a, score_b, score_c, prob,
    acc, sent, mix, got,
    load, store, gather_send, gather_recv, back_send, mix_recv, back_recv, relay_send,
):
    rows = query.shape[0]
    scale = ATT_DIM ** -0.5
    me = lax.axis_index("seq")
    odd = lax.rem(me, 2)
    pair = me + 1 - 2 * odd
    far = span // 2
    square = n == 8
    chip = me // 2

    def sends(which, j):
        there = me + 2 * j < n
        return there & (chip != 1) if square and which == DK and j == 1 else there
    score = (score_a, score_b, score_c)

    def load_kv(g, which):
        columns = pl.ds(pl.multiple_of(g * ATT_DIM, ATT_DIM), ATT_DIM)
        source = (keys, values)[which]
        return pltpu.make_async_copy(
            source.at[:, columns], kv.at[g, 0, which], load.at[2 + 2 * g + which]
        )

    def start_load(g, _):
        load_kv(g, 0).start()
        load_kv(g, 1).start()
        return 0

    lax.fori_loop(0, kv_count, start_load, 0)
    load_query = pltpu.make_async_copy(query_hbm, query, load.at[0])
    load_grad = pltpu.make_async_copy(grad_hbm, grad, load.at[1])
    load_query.start()
    load_grad.start()

    def signal(barrier, target):
        pl.semaphore_signal(barrier, inc=1, device_id={"seq": target}, device_id_type=MESH)

    barrier = pltpu.get_barrier_semaphore()
    signal(barrier, pair)
    for j in range(1, far + 1):
        @pl.when(me + 2 * j < n)
        def _():
            signal(barrier, me + 2 * j)

        @pl.when(me - 2 * j >= 0)
        def _():
            signal(barrier, me - 2 * j)

    def clear(g, _):
        for k in range(1, span):
            @pl.when(me - k < 0)
            def _():
                kv[g, k] = jnp.zeros((2, rows, ATT_DIM), BF16)
        return 0

    lax.fori_loop(0, kv_count, clear, 0)
    q_lane = lax.broadcasted_iota(jnp.int32, (1, rows), 1)
    position = q_lane + me * rows
    start = jnp.zeros((1, rows), jnp.int32)
    end = 0
    for i in range(lengths.shape[0]):
        end = end + lengths[i]
        start = jnp.where(position >= end, end, start)

    k_row = lax.broadcasted_iota(jnp.int32, (rows, rows), 0)
    for k in range(span):
        allow = k_row >= start - (me - k) * rows
        if k == 0:
            allow = allow & (k_row <= q_lane)
        bias[k * rows:(k + 1) * rows, :] = jnp.where(allow, 0.0, MASKED)
    value_t[ATT_DIM:, :] = jnp.ones((ONES, value_t.shape[1]), BF16)
    pl.semaphore_wait(
        barrier, 1 + jnp.minimum(me // 2, far) + jnp.minimum((n - 1 - me) // 2, far)
    )

    def remote(source, target, send_sem, recv_sem, device):
        return pltpu.make_async_remote_copy(
            src_ref=source, dst_ref=target, send_sem=send_sem, recv_sem=recv_sem,
            device_id={"seq": device}, device_id_type=MESH,
        )

    def gather(g, which, j):
        return remote(
            kv.at[g, 0, which], kv.at[g, 2 * j, which], gather_send.at[g, which, 2 * j],
            gather_recv.at[g, which, 2 * j], me + 2 * j,
        )

    def hand_on(g, which, j, slot):
        return remote(
            kv.at[g, 2 * j, which], kv.at[g, slot, which], gather_send.at[g, which, slot],
            gather_recv.at[g, which, slot], pair,
        )

    def each_hand_on(first, last, act):
        for j in range(first, last + 1):
            if j >= 1:
                @pl.when((odd == 1) & (me - 2 * j >= 0))
                def _():
                    act(j, 2 * j - 1)
            if j < far:
                @pl.when((odd == 0) & (me - 2 * j >= 0))
                def _():
                    act(j, 2 * j + 1)

    def begin(g):
        for which in (DK, DV):
            for j in range(far, 0, -1):
                @pl.when(sends(which, j))
                def _():
                    gather(g, which, j).start()
            each_hand_on(0, 0, lambda j, slot: hand_on(g, which, j, slot).start())

    load_kv(0, DK).wait()
    load_kv(0, DV).wait()
    begin(0)

    def relay(g):
        return remote(
            kv.at[g, 4, DK], kv.at[g, 2, DK], relay_send.at[g],
            gather_recv.at[g, DK, 2], me - 2,
        )

    def pass_on(g, which):
        for j in range(far, 0, -1):
            @pl.when(me - 2 * j >= 0)
            def _():
                gather(g, which, j).wait_recv()

            if square and which == DK and j == 2:
                @pl.when(chip == 3)
                def _():
                    relay(g).start()
            each_hand_on(j, j, lambda j, slot: hand_on(g, which, j, slot).start())

    def handed(g, which):
        for k in range(1, span, 2):
            @pl.when(me - k >= 0)
            def _():
                hand_on(g, which, 0, k).wait_recv()

    def partial(g, which, k):
        part = acc[g, which, :, k * rows:(k + 1) * rows]
        return part * (1.0 / scale) if which == DV else part

    def to_pair(g, which, k, j):
        return remote(
            sent.at[g, which, k], mix.at[g, which, j], back_send.at[g, which, k],
            mix_recv.at[g, which, j], pair,
        )

    def back(g, which, j):
        return remote(
            sent.at[g, which, 2 * j], got.at[g, which, j], back_send.at[g, which, 2 * j],
            back_recv.at[g, which, j], me - 2 * j,
        )

    def each_to_pair(act):
        for k in range(1, span, 2):
            @pl.when((odd == 1) & (me - k >= 0))
            def _():
                act(k, (k - 1) // 2)

            @pl.when((odd == 0) & (me - k >= 0))
            def _():
                act(k, (k + 1) // 2)

    def share_partial(g, which):
        def act(k, j):
            sent[g, which, k] = partial(g, which, k).astype(BF16)
            to_pair(g, which, k, j).start()

        each_to_pair(act)

    def wait_mix(g, which, j):
        to_pair(g, which, 1, j).wait_recv()

    def combine(g, which):
        for j in range(far, 0, -1):
            def give(mixed):
                part = partial(g, which, 2 * j)
                if mixed:
                    wait_mix(g, which, j)
                    part = part + mix[g, which, j].astype(F32)
                sent[g, which, 2 * j] = part.astype(BF16)
                back(g, which, j).start()

            if j < far:
                @pl.when(me - 2 * j >= 0)
                def _():
                    give(True)
            else:
                @pl.when((me - 2 * j >= 0) & (odd == 1))
                def _():
                    give(True)

                @pl.when((me - 2 * j >= 0) & (odd == 0))
                def _():
                    give(False)

    def at(k):
        return slice(k * rows, (k + 1) * rows)

    for g in range(1, kv_count):
        load_kv(g, DK).wait()
        load_kv(g, DV).wait()
    load_query.wait()
    load_grad.wait()

    def near(i, _):
        for u in range(4):
            h = 4 * i + u
            g = h // share
            columns = pl.ds(pl.multiple_of(h * ATT_DIM, ATT_DIM), ATT_DIM)
            query_t[h] = query[:, columns].T
            cot_t[h] = grad[:, columns].T
            s = lax.dot_general(kv[g, 0, 0], query_t[h], NN, preferred_element_type=F32)
            s = s + bias[at(0), :]
            near_score[h] = s
            most = s[:FOLD]
            for r in range(FOLD, rows, FOLD):
                most = jnp.maximum(most, s[r:r + FOLD])
            near_top[h] = most
            near_slope[h] = lax.dot_general(
                kv[g, 0, 1], cot_t[h], NN, preferred_element_type=F32
            )
        return 0

    lax.fori_loop(0, kv_count * share // 4, near, 0)
    pass_on(0, DK)
    pass_on(0, DV)

    def group(g, _):
        handed(g, DK)
        handed(g, DV)
        for k in range(span):
            key_t[:, at(k)] = kv[g, k, 0].T
            value_t[:ATT_DIM, at(k)] = kv[g, k, 1].T
        if kv_count > 1:
            @pl.when(g + 1 < kv_count)
            def _():
                begin(g + 1)

        def columns(h):
            return pl.ds(pl.multiple_of((g * share + h) * ATT_DIM, ATT_DIM), ATT_DIM)

        def add(which, h, k, a, b):
            part = lax.dot_general(a, b, NT, preferred_element_type=F32)
            if h:
                part = acc[g, which, :, at(k)] + part
            acc[g, which, :, at(k)] = part

        def scores(h, slot):
            most = near_top[g * share + h]
            for k in range(1, span):
                s = lax.dot_general(
                    kv[g, k, 0], query_t[g * share + h], NN, preferred_element_type=F32
                )
                s = s + bias[at(k), :]
                score[slot][at(k - 1), :] = s
                for r in range(0, rows, FOLD):
                    most = jnp.maximum(most, s[r:r + FOLD])
                yield
            top[slot] = jnp.max(most, axis=0, keepdims=True)

        def softmax(h, slot):
            peak = top[slot]
            out_t = jnp.zeros((ATT_DIM + ONES, rows), F32)
            for k in range(span):
                s = score[slot][at(k - 1), :] if k else near_score[g * share + h]
                p = jnp.exp2((s - peak) * (scale * LOG2E)).astype(BF16)
                prob[h, at(k), :] = p
                out_t = out_t + lax.dot_general(
                    value_t[:, at(k)], p, NN, preferred_element_type=F32
                )
                yield
            inverse = 1.0 / out_t[ATT_DIM:ATT_DIM + 1]
            out_t = out_t[:ATT_DIM] * inverse
            out[:, columns(h)] = out_t.astype(BF16).T
            factor = inverse * scale
            factors[h] = factor
            g_t = cot_t[g * share + h].astype(F32) * factor
            delta[h] = jnp.sum(g_t * out_t, axis=0, keepdims=True)
            grad_t[h] = g_t.astype(BF16)

        def value_sums(h):
            for k in range(span):
                add(DV, h, k, grad_t[h], prob[h, at(k), :])
                yield

        def slopes(h, slot):
            for k in range(1, span):
                score[slot][at(k - 1), :] = lax.dot_general(
                    kv[g, k, 1], grad_t[h], NN, preferred_element_type=F32
                )
                yield

        def key_sums(h, slot):
            low = delta[h]
            dq = jnp.zeros((ATT_DIM, rows), F32)
            for k in range(span):
                if k:
                    dp = score[slot][at(k - 1), :]
                else:
                    dp = near_slope[g * share + h] * factors[h]
                ds = prob[h, at(k), :] * (dp - low).astype(BF16)
                dq = dq + lax.dot_general(key_t[:, at(k)], ds, NN, preferred_element_type=F32)
                add(DK, h, k, query_t[g * share + h], ds)
                yield
            query_grad[:, columns(h)] = dq.astype(BF16).T

        def ahead(h):
            if h < share:
                return scores(h, h % 3)
            return slopes(h - share, h % 3)

        half = share // 2
        interleave(ahead(0), ahead(1))
        for h in range(share):
            runs = [softmax(h, h % 3), ahead(h + 2)]
            if h > 1:
                runs.append(value_sums(h - 2))
            interleave(*runs)
        interleave(value_sums(share - 2), value_sums(share - 1))
        share_partial(g, DV)
        store_heads(0, g).start()
        if kv_count > 1:
            @pl.when(g >= 1)
            def _():
                combine(g - 1, DK)
        for h in range(share):
            if h == half:
                combine(g, DV)
                if kv_count > 1:
                    @pl.when(g + 1 < kv_count)
                    def _():
                        pass_on(g + 1, DK)
                        pass_on(g + 1, DV)
            runs = [key_sums(h, (h + share) % 3)]
            if h + 2 < share:
                runs.append(slopes(h + 2, (h + 2 + share) % 3))
            interleave(*runs)
        store_heads(1, g).start()
        share_partial(g, DK)
        return 0

    def store_heads(which, g):
        wide = share * ATT_DIM
        columns = pl.ds(pl.multiple_of(g * wide, wide), wide)
        source, target = ((out, out_hbm), (query_grad, query_grad_hbm))[which]
        return pltpu.make_async_copy(
            source.at[:, columns], target.at[:, columns], store.at[which, g]
        )

    lax.fori_loop(0, kv_count, group, 0)
    combine(kv_count - 1, DK)
    def finish(g, _):
        columns = pl.ds(pl.multiple_of(g * ATT_DIM, ATT_DIM), ATT_DIM)
        for which, target in ((DV, value_grad), (DK, key_grad)):
            unit = scale if which == DV else 1.0

            @pl.when(odd == 0)
            def _():
                wait_mix(g, which, 0)
                acc[g, which, :, 0:rows] += mix[g, which, 0].astype(F32) * unit

            for j in range(1, far + 1):
                @pl.when(me + 2 * j < n)
                def _():
                    back(g, which, j).wait_recv()
                    acc[g, which, :, 0:rows] += got[g, which, j].astype(F32) * unit
            target[:, columns] = partial(g, which, 0).T.astype(BF16)
            for j in range(1, far + 1):
                @pl.when(me - 2 * j >= 0)
                def _():
                    back(g, which, j).wait_send()
            each_to_pair(lambda k, j: to_pair(g, which, k, j).wait_send())
        for which in (DK, DV):
            for j in range(1, far + 1):
                @pl.when(sends(which, j))
                def _():
                    gather(g, which, j).wait_send()
            each_hand_on(
                0, far, lambda j, slot: hand_on(g, which, j, slot).wait_send()
            )
            store_heads(which, g).wait()
        if square:
            @pl.when(chip == 3)
            def _():
                relay(g).wait_send()
        return 0

    lax.fori_loop(0, kv_count, finish, 0)


def deliver(*refs):
    sources, targets, buffers = refs[:4], refs[4:8], refs[8:12]
    first, second = refs[12], refs[13]
    parts = []
    for i in range(4):
        rows = sources[i].shape[0]
        cuts = 4 if i < 2 else 1
        for c in range(cuts):
            at = pl.ds(c * rows // cuts, rows // cuts)
            m = len(parts)
            parts.append((
                pltpu.make_async_copy(sources[i].at[at], buffers[i].at[at], first.at[m]),
                pltpu.make_async_copy(buffers[i].at[at], targets[i].at[at], second.at[m]),
            ))
    for fetch, _ in parts:
        fetch.start()
    for fetch, write in parts:
        fetch.wait()
        write.start()
    for _, write in parts:
        write.wait()


def on_device(lengths, query, keys, values, attention_grad):
    n = lax.axis_size("seq")
    rows = query.shape[0]
    kv_count = keys.shape[1] // ATT_DIM
    share = query.shape[1] // keys.shape[1]
    span = n // 2 + 1
    whole = pl.BlockSpec(memory_space=pltpu.VMEM)
    hbm = pl.BlockSpec(memory_space=pltpu.HBM)
    keyed = span * rows
    turned = (ATT_DIM, rows)
    results = pl.pallas_call(
        functools.partial(kernel, n, span, kv_count, share),
        out_shape=[
            jax.ShapeDtypeStruct(a.shape, BF16) for a in (query, query, keys, values)
        ],
        in_specs=[pl.BlockSpec(memory_space=pltpu.SMEM)]
        + [pl.BlockSpec(memory_space=pl.ANY)] * 4,
        out_specs=[pl.BlockSpec(memory_space=pl.ANY)] * 2 + [whole] * 2,
        scratch_shapes=[
            pltpu.VMEM(query.shape, BF16),
            pltpu.VMEM(query.shape, BF16),
            pltpu.VMEM(query.shape, BF16),
            pltpu.VMEM(query.shape, BF16),
            pltpu.VMEM((kv_count, span, 2, rows, ATT_DIM), BF16),
            pltpu.VMEM((ATT_DIM, keyed), BF16),
            pltpu.VMEM((ATT_DIM + ONES, keyed), BF16),
            pltpu.VMEM((kv_count * share,) + turned, BF16),
            pltpu.VMEM((kv_count * share,) + turned, BF16),
            pltpu.VMEM((share,) + turned, BF16),
            pltpu.VMEM((share, 1, rows), F32),
            pltpu.VMEM((share, 1, rows), F32),
            pltpu.VMEM((3, 1, rows), F32),
            pltpu.VMEM((kv_count * share, FOLD, rows), F32),
            pltpu.VMEM((kv_count * share, rows, rows), F32),
            pltpu.VMEM((kv_count * share, rows, rows), F32),
            pltpu.VMEM((keyed, rows), F32),
            pltpu.VMEM((keyed, rows), F32),
            pltpu.VMEM((keyed, rows), F32),
            pltpu.VMEM((keyed, rows), F32),
            pltpu.VMEM((share, keyed, rows), BF16),
            pltpu.VMEM((kv_count, 2, ATT_DIM, keyed), F32),
            pltpu.VMEM((kv_count, 2, span) + turned, BF16),
            pltpu.VMEM((kv_count, 2, span // 2 + 1) + turned, BF16),
            pltpu.VMEM((kv_count, 2, span // 2 + 1) + turned, BF16),
            pltpu.SemaphoreType.DMA((2 + 2 * kv_count,)),
            pltpu.SemaphoreType.DMA((2, kv_count)),
            pltpu.SemaphoreType.DMA((kv_count, 2, span)),
            pltpu.SemaphoreType.DMA((kv_count, 2, span)),
            pltpu.SemaphoreType.DMA((kv_count, 2, span)),
            pltpu.SemaphoreType.DMA((kv_count, 2, span // 2 + 1)),
            pltpu.SemaphoreType.DMA((kv_count, 2, span // 2 + 1)),
            pltpu.SemaphoreType.DMA((kv_count,)),
        ],
        compiler_params=pltpu.CompilerParams(
            collective_id=0, has_side_effects=True, vmem_limit_bytes=60 << 20
        ),
    )(lengths, query, keys, values, attention_grad)
    return pl.pallas_call(
        deliver,
        out_shape=[jax.ShapeDtypeStruct(a.shape, BF16) for a in results],
        in_specs=[hbm] * 4,
        out_specs=[hbm] * 4,
        scratch_shapes=[pltpu.VMEM(a.shape, BF16) for a in results]
        + [pltpu.SemaphoreType.DMA((10,)), pltpu.SemaphoreType.DMA((10,))],
    )(*results)


def solution(mesh):
    in_specs = (P(), P("seq", "head"), P("seq", "head"), P("seq", "head"), P("seq", "head"))
    out_specs = (P("seq", "head"), P("seq", "head"), P("seq", "head"), P("seq", "head"))
    return jax.shard_map(
        on_device, mesh=mesh, in_specs=in_specs, out_specs=out_specs, check_vma=False
    )
```

```python
import functools

import jax
import jax.numpy as jnp
from jax import lax
from jax.experimental import pallas as pl
from jax.experimental.pallas import tpu as pltpu
from jax.sharding import PartitionSpec as P

ATT_DIM = 128
LOG2E = 1.4426950408889634
MASKED = -1.0e30
MESH = pl.DeviceIdType.MESH

F32 = jnp.float32
BF16 = jnp.bfloat16
NT = (((1,), (1,)), ((), ()))
NN = (((1,), (0,)), ((), ()))
DK, DV = 0, 1
ONES = 16
FOLD = 32


def interleave(*runs):
    runs = list(runs)
    while runs:
        runs = [run for run in runs if next(run, True) is None]


def kernel(
    n, span, kv_count, share,
    lengths, query_hbm, keys, values, grad_hbm,
    out_hbm, query_grad_hbm, key_grad, value_grad,
    query, grad, out, query_grad, kv, key_t, value_t, query_t, cot_t, grad_t, delta, factors,
    top, near_top, near_score, near_slope, bias, score_a, score_b, score_c, prob,
    acc, sent, mix, got,
    load, store, gather_send, gather_recv, back_send, mix_recv, back_recv, relay_send,
):
    rows = query.shape[0]
    scale = ATT_DIM ** -0.5
    me = lax.axis_index("seq")
    odd = lax.rem(me, 2)
    pair = me + 1 - 2 * odd
    far = span // 2
    square = n == 8
    chip = me // 2

    def sends(which, j):
        there = me + 2 * j < n
        return there & (chip != 1) if square and which == DK and j == 1 else there
    score = (score_a, score_b, score_c)

    def load_kv(g, which):
        columns = pl.ds(pl.multiple_of(g * ATT_DIM, ATT_DIM), ATT_DIM)
        source = (keys, values)[which]
        return pltpu.make_async_copy(
            source.at[:, columns], kv.at[g, 0, which], load.at[2 + 2 * g + which]
        )

    def start_load(g, _):
        load_kv(g, 0).start()
        load_kv(g, 1).start()
        return 0

    lax.fori_loop(0, kv_count, start_load, 0)
    load_query = pltpu.make_async_copy(query_hbm, query, load.at[0])
    load_grad = pltpu.make_async_copy(grad_hbm, grad, load.at[1])
    load_query.start()
    load_grad.start()

    def signal(barrier, target):
        pl.semaphore_signal(barrier, inc=1, device_id={"seq": target}, device_id_type=MESH)

    barrier = pltpu.get_barrier_semaphore()
    signal(barrier, pair)
    for j in range(1, far + 1):
        @pl.when(me + 2 * j < n)
        def _():
            signal(barrier, me + 2 * j)

        @pl.when(me - 2 * j >= 0)
        def _():
            signal(barrier, me - 2 * j)

    def clear(g, _):
        for k in range(1, span):
            @pl.when(me - k < 0)
            def _():
                kv[g, k] = jnp.zeros((2, rows, ATT_DIM), BF16)
        return 0

    lax.fori_loop(0, kv_count, clear, 0)
    q_lane = lax.broadcasted_iota(jnp.int32, (1, rows), 1)
    position = q_lane + me * rows
    start = jnp.zeros((1, rows), jnp.int32)
    end = 0
    for i in range(lengths.shape[0]):
        end = end + lengths[i]
        start = jnp.where(position >= end, end, start)

    k_row = lax.broadcasted_iota(jnp.int32, (rows, rows), 0)
    for k in range(span):
        allow = k_row >= start - (me - k) * rows
        if k == 0:
            allow = allow & (k_row <= q_lane)
        bias[k * rows:(k + 1) * rows, :] = jnp.where(allow, 0.0, MASKED)
    value_t[ATT_DIM:, :] = jnp.ones((ONES, value_t.shape[1]), BF16)
    pl.semaphore_wait(
        barrier, 1 + jnp.minimum(me // 2, far) + jnp.minimum((n - 1 - me) // 2, far)
    )

    def remote(source, target, send_sem, recv_sem, device):
        return pltpu.make_async_remote_copy(
            src_ref=source, dst_ref=target, send_sem=send_sem, recv_sem=recv_sem,
            device_id={"seq": device}, device_id_type=MESH,
        )

    def gather(g, which, j):
        return remote(
            kv.at[g, 0, which], kv.at[g, 2 * j, which], gather_send.at[g, which, 2 * j],
            gather_recv.at[g, which, 2 * j], me + 2 * j,
        )

    def hand_on(g, which, j, slot):
        return remote(
            kv.at[g, 2 * j, which], kv.at[g, slot, which], gather_send.at[g, which, slot],
            gather_recv.at[g, which, slot], pair,
        )

    def each_hand_on(first, last, act):
        for j in range(first, last + 1):
            if j >= 1:
                @pl.when((odd == 1) & (me - 2 * j >= 0))
                def _():
                    act(j, 2 * j - 1)
            if j < far:
                @pl.when((odd == 0) & (me - 2 * j >= 0))
                def _():
                    act(j, 2 * j + 1)

    def begin(g):
        for which in (DK, DV):
            for j in range(far, 0, -1):
                @pl.when(sends(which, j))
                def _():
                    gather(g, which, j).start()
            each_hand_on(0, 0, lambda j, slot: hand_on(g, which, j, slot).start())

    load_kv(0, DK).wait()
    load_kv(0, DV).wait()
    begin(0)

    def relay(g):
        return remote(
            kv.at[g, 4, DK], kv.at[g, 2, DK], relay_send.at[g],
            gather_recv.at[g, DK, 2], me - 2,
        )

    def relay_keys(g):
        if square:
            @pl.when(chip == 3)
            def _():
                gather(g, DK, 2).wait_recv()
                relay(g).start()

    def pass_on(g, which):
        for j in range(far, 0, -1):
            there = me - 2 * j >= 0
            if square and which == DK and j == 2:
                there = there & (chip != 3)

            @pl.when(there)
            def _():
                gather(g, which, j).wait_recv()
            each_hand_on(j, j, lambda j, slot: hand_on(g, which, j, slot).start())

    def handed(g, which):
        for k in range(1, span, 2):
            @pl.when(me - k >= 0)
            def _():
                hand_on(g, which, 0, k).wait_recv()

    def partial(g, which, k):
        part = acc[g, which, :, k * rows:(k + 1) * rows]
        return part * (1.0 / scale) if which == DV else part

    def to_pair(g, which, k, j):
        return remote(
            sent.at[g, which, k], mix.at[g, which, j], back_send.at[g, which, k],
            mix_recv.at[g, which, j], pair,
        )

    def back(g, which, j):
        return remote(
            sent.at[g, which, 2 * j], got.at[g, which, j], back_send.at[g, which, 2 * j],
            back_recv.at[g, which, j], me - 2 * j,
        )

    def each_to_pair(act):
        for k in range(1, span, 2):
            @pl.when((odd == 1) & (me - k >= 0))
            def _():
                act(k, (k - 1) // 2)

            @pl.when((odd == 0) & (me - k >= 0))
            def _():
                act(k, (k + 1) // 2)

    def share_partial(g, which):
        def act(k, j):
            sent[g, which, k] = partial(g, which, k).astype(BF16)
            to_pair(g, which, k, j).start()

        each_to_pair(act)

    def wait_mix(g, which, j):
        to_pair(g, which, 1, j).wait_recv()

    def combine(g, which):
        for j in range(far, 0, -1):
            def give(mixed):
                part = partial(g, which, 2 * j)
                if mixed:
                    wait_mix(g, which, j)
                    part = part + mix[g, which, j].astype(F32)
                sent[g, which, 2 * j] = part.astype(BF16)
                back(g, which, j).start()

            if j < far:
                @pl.when(me - 2 * j >= 0)
                def _():
                    give(True)
            else:
                @pl.when((me - 2 * j >= 0) & (odd == 1))
                def _():
                    give(True)

                @pl.when((me - 2 * j >= 0) & (odd == 0))
                def _():
                    give(False)

    def at(k):
        return slice(k * rows, (k + 1) * rows)

    for g in range(1, kv_count):
        load_kv(g, DK).wait()
        load_kv(g, DV).wait()
    load_query.wait()
    load_grad.wait()

    def near(i, _):
        for u in range(4):
            h = 4 * i + u
            g = h // share
            columns = pl.ds(pl.multiple_of(h * ATT_DIM, ATT_DIM), ATT_DIM)
            query_t[h] = query[:, columns].T
            cot_t[h] = grad[:, columns].T
            s = lax.dot_general(kv[g, 0, 0], query_t[h], NN, preferred_element_type=F32)
            s = s + bias[at(0), :]
            near_score[h] = s
            most = s[:FOLD]
            for r in range(FOLD, rows, FOLD):
                most = jnp.maximum(most, s[r:r + FOLD])
            near_top[h] = most
            near_slope[h] = lax.dot_general(
                kv[g, 0, 1], cot_t[h], NN, preferred_element_type=F32
            )
        return 0

    lax.fori_loop(0, kv_count * share // 4, near, 0)
    relay_keys(0)
    pass_on(0, DK)
    pass_on(0, DV)

    def group(g, _):
        handed(g, DK)
        handed(g, DV)
        for k in range(span):
            key_t[:, at(k)] = kv[g, k, 0].T
            value_t[:ATT_DIM, at(k)] = kv[g, k, 1].T
        if kv_count > 1:
            @pl.when(g + 1 < kv_count)
            def _():
                begin(g + 1)

        def columns(h):
            return pl.ds(pl.multiple_of((g * share + h) * ATT_DIM, ATT_DIM), ATT_DIM)

        def add(which, h, k, a, b):
            part = lax.dot_general(a, b, NT, preferred_element_type=F32)
            if h:
                part = acc[g, which, :, at(k)] + part
            acc[g, which, :, at(k)] = part

        def scores(h, slot):
            most = near_top[g * share + h]
            for k in range(1, span):
                s = lax.dot_general(
                    kv[g, k, 0], query_t[g * share + h], NN, preferred_element_type=F32
                )
                s = s + bias[at(k), :]
                score[slot][at(k - 1), :] = s
                for r in range(0, rows, FOLD):
                    most = jnp.maximum(most, s[r:r + FOLD])
                yield
            top[slot] = jnp.max(most, axis=0, keepdims=True)

        def softmax(h, slot):
            peak = top[slot]
            out_t = jnp.zeros((ATT_DIM + ONES, rows), F32)
            for k in range(span):
                s = score[slot][at(k - 1), :] if k else near_score[g * share + h]
                p = jnp.exp2((s - peak) * (scale * LOG2E)).astype(BF16)
                prob[h, at(k), :] = p
                out_t = out_t + lax.dot_general(
                    value_t[:, at(k)], p, NN, preferred_element_type=F32
                )
                yield
            inverse = 1.0 / out_t[ATT_DIM:ATT_DIM + 1]
            out_t = out_t[:ATT_DIM] * inverse
            out[:, columns(h)] = out_t.astype(BF16).T
            factor = inverse * scale
            factors[h] = factor
            g_t = cot_t[g * share + h].astype(F32) * factor
            delta[h] = jnp.sum(g_t * out_t, axis=0, keepdims=True)
            grad_t[h] = g_t.astype(BF16)

        def value_sums(h):
            for k in range(span):
                add(DV, h, k, grad_t[h], prob[h, at(k), :])
                yield

        def slopes(h, slot):
            for k in range(1, span):
                score[slot][at(k - 1), :] = lax.dot_general(
                    kv[g, k, 1], grad_t[h], NN, preferred_element_type=F32
                )
                yield

        def key_sums(h, slot):
            low = delta[h]
            dq = jnp.zeros((ATT_DIM, rows), F32)
            for k in range(span):
                if k:
                    dp = score[slot][at(k - 1), :]
                else:
                    dp = near_slope[g * share + h] * factors[h]
                ds = prob[h, at(k), :] * (dp - low).astype(BF16)
                dq = dq + lax.dot_general(key_t[:, at(k)], ds, NN, preferred_element_type=F32)
                add(DK, h, k, query_t[g * share + h], ds)
                yield
            query_grad[:, columns(h)] = dq.astype(BF16).T

        def ahead(h):
            if h < share:
                return scores(h, h % 3)
            return slopes(h - share, h % 3)

        half = share // 2
        interleave(ahead(0), ahead(1))
        for h in range(share):
            runs = [softmax(h, h % 3), ahead(h + 2)]
            if h > 1:
                runs.append(value_sums(h - 2))
            interleave(*runs)
        interleave(value_sums(share - 2), value_sums(share - 1))
        share_partial(g, DV)
        store_heads(0, g).start()
        if kv_count > 1:
            @pl.when(g + 1 < kv_count)
            def _():
                relay_keys(g + 1)

            @pl.when(g >= 1)
            def _():
                combine(g - 1, DK)
        for h in range(share):
            if h == half:
                combine(g, DV)
                if kv_count > 1:
                    @pl.when(g + 1 < kv_count)
                    def _():
                        pass_on(g + 1, DK)
                        pass_on(g + 1, DV)
            runs = [key_sums(h, (h + share) % 3)]
            if h + 2 < share:
                runs.append(slopes(h + 2, (h + 2 + share) % 3))
            interleave(*runs)
        store_heads(1, g).start()
        share_partial(g, DK)
        return 0

    def store_heads(which, g):
        wide = share * ATT_DIM
        columns = pl.ds(pl.multiple_of(g * wide, wide), wide)
        source, target = ((out, out_hbm), (query_grad, query_grad_hbm))[which]
        return pltpu.make_async_copy(
            source.at[:, columns], target.at[:, columns], store.at[which, g]
        )

    lax.fori_loop(0, kv_count, group, 0)
    combine(kv_count - 1, DK)
    def finish(g, _):
        columns = pl.ds(pl.multiple_of(g * ATT_DIM, ATT_DIM), ATT_DIM)
        for which, target in ((DV, value_grad), (DK, key_grad)):
            unit = scale if which == DV else 1.0

            @pl.when(odd == 0)
            def _():
                wait_mix(g, which, 0)
                acc[g, which, :, 0:rows] += mix[g, which, 0].astype(F32) * unit

            for j in range(1, far + 1):
                @pl.when(me + 2 * j < n)
                def _():
                    back(g, which, j).wait_recv()
                    acc[g, which, :, 0:rows] += got[g, which, j].astype(F32) * unit
            target[:, columns] = partial(g, which, 0).T.astype(BF16)
            for j in range(1, far + 1):
                @pl.when(me - 2 * j >= 0)
                def _():
                    back(g, which, j).wait_send()
            each_to_pair(lambda k, j: to_pair(g, which, k, j).wait_send())
        for which in (DK, DV):
            for j in range(1, far + 1):
                @pl.when(sends(which, j))
                def _():
                    gather(g, which, j).wait_send()
            each_hand_on(
                0, far, lambda j, slot: hand_on(g, which, j, slot).wait_send()
            )
            store_heads(which, g).wait()
        if square:
            @pl.when(chip == 3)
            def _():
                relay(g).wait_send()
        return 0

    lax.fori_loop(0, kv_count, finish, 0)


def deliver(*refs):
    sources, targets, buffers = refs[:4], refs[4:8], refs[8:12]
    first, second = refs[12], refs[13]
    parts = []
    for i in range(4):
        rows = sources[i].shape[0]
        cuts = 4 if i < 2 else 1
        for c in range(cuts):
            at = pl.ds(c * rows // cuts, rows // cuts)
            m = len(parts)
            parts.append((
                pltpu.make_async_copy(sources[i].at[at], buffers[i].at[at], first.at[m]),
                pltpu.make_async_copy(buffers[i].at[at], targets[i].at[at], second.at[m]),
            ))
    for fetch, _ in parts:
        fetch.start()
    for fetch, write in parts:
        fetch.wait()
        write.start()
    for _, write in parts:
        write.wait()


def on_device(lengths, query, keys, values, attention_grad):
    n = lax.axis_size("seq")
    rows = query.shape[0]
    kv_count = keys.shape[1] // ATT_DIM
    share = query.shape[1] // keys.shape[1]
    span = n // 2 + 1
    whole = pl.BlockSpec(memory_space=pltpu.VMEM)
    hbm = pl.BlockSpec(memory_space=pltpu.HBM)
    keyed = span * rows
    turned = (ATT_DIM, rows)
    results = pl.pallas_call(
        functools.partial(kernel, n, span, kv_count, share),
        out_shape=[
            jax.ShapeDtypeStruct(a.shape, BF16) for a in (query, query, keys, values)
        ],
        in_specs=[pl.BlockSpec(memory_space=pltpu.SMEM)]
        + [pl.BlockSpec(memory_space=pl.ANY)] * 4,
        out_specs=[pl.BlockSpec(memory_space=pl.ANY)] * 2 + [whole] * 2,
        scratch_shapes=[
            pltpu.VMEM(query.shape, BF16),
            pltpu.VMEM(query.shape, BF16),
            pltpu.VMEM(query.shape, BF16),
            pltpu.VMEM(query.shape, BF16),
            pltpu.VMEM((kv_count, span, 2, rows, ATT_DIM), BF16),
            pltpu.VMEM((ATT_DIM, keyed), BF16),
            pltpu.VMEM((ATT_DIM + ONES, keyed), BF16),
            pltpu.VMEM((kv_count * share,) + turned, BF16),
            pltpu.VMEM((kv_count * share,) + turned, BF16),
            pltpu.VMEM((share,) + turned, BF16),
            pltpu.VMEM((share, 1, rows), F32),
            pltpu.VMEM((share, 1, rows), F32),
            pltpu.VMEM((3, 1, rows), F32),
            pltpu.VMEM((kv_count * share, FOLD, rows), F32),
            pltpu.VMEM((kv_count * share, rows, rows), F32),
            pltpu.VMEM((kv_count * share, rows, rows), F32),
            pltpu.VMEM((keyed, rows), F32),
            pltpu.VMEM((keyed, rows), F32),
            pltpu.VMEM((keyed, rows), F32),
            pltpu.VMEM((keyed, rows), F32),
            pltpu.VMEM((share, keyed, rows), BF16),
            pltpu.VMEM((kv_count, 2, ATT_DIM, keyed), F32),
            pltpu.VMEM((kv_count, 2, span) + turned, BF16),
            pltpu.VMEM((kv_count, 2, span // 2 + 1) + turned, BF16),
            pltpu.VMEM((kv_count, 2, span // 2 + 1) + turned, BF16),
            pltpu.SemaphoreType.DMA((2 + 2 * kv_count,)),
            pltpu.SemaphoreType.DMA((2, kv_count)),
            pltpu.SemaphoreType.DMA((kv_count, 2, span)),
            pltpu.SemaphoreType.DMA((kv_count, 2, span)),
            pltpu.SemaphoreType.DMA((kv_count, 2, span)),
            pltpu.SemaphoreType.DMA((kv_count, 2, span // 2 + 1)),
            pltpu.SemaphoreType.DMA((kv_count, 2, span // 2 + 1)),
            pltpu.SemaphoreType.DMA((kv_count,)),
        ],
        compiler_params=pltpu.CompilerParams(
            collective_id=0, has_side_effects=True, vmem_limit_bytes=60 << 20
        ),
    )(lengths, query, keys, values, attention_grad)
    return pl.pallas_call(
        deliver,
        out_shape=[jax.ShapeDtypeStruct(a.shape, BF16) for a in results],
        in_specs=[hbm] * 4,
        out_specs=[hbm] * 4,
        scratch_shapes=[pltpu.VMEM(a.shape, BF16) for a in results]
        + [pltpu.SemaphoreType.DMA((10,)), pltpu.SemaphoreType.DMA((10,))],
    )(*results)


def solution(mesh):
    in_specs = (P(), P("seq", "head"), P("seq", "head"), P("seq", "head"), P("seq", "head"))
    out_specs = (P("seq", "head"), P("seq", "head"), P("seq", "head"), P("seq", "head"))
    return jax.shard_map(
        on_device, mesh=mesh, in_specs=in_specs, out_specs=out_specs, check_vma=False
    )
```

```python
import functools

import jax
import jax.numpy as jnp
from jax import lax
from jax.experimental import pallas as pl
from jax.experimental.pallas import tpu as pltpu
from jax.sharding import PartitionSpec as P

ATT_DIM = 128
LOG2E = 1.4426950408889634
MASKED = -1.0e30
MESH = pl.DeviceIdType.MESH

F32 = jnp.float32
BF16 = jnp.bfloat16
NT = (((1,), (1,)), ((), ()))
NN = (((1,), (0,)), ((), ()))
DK, DV = 0, 1
ONES = 16
FOLD = 32


def interleave(*runs):
    runs = list(runs)
    while runs:
        runs = [run for run in runs if next(run, True) is None]


def kernel(
    n, span, kv_count, share,
    lengths, query_hbm, keys, values, grad_hbm,
    out_hbm, query_grad_hbm, key_grad, value_grad,
    query, grad, out, query_grad, kv, key_t, value_t, query_t, cot_t, grad_t, delta, factors,
    top, near_top, near_score, near_slope, bias, score_a, score_b, score_c, prob,
    acc, sent, mix, got,
    load, store, gather_send, gather_recv, back_send, mix_recv, back_recv, relay_send,
):
    rows = query.shape[0]
    scale = ATT_DIM ** -0.5
    me = lax.axis_index("seq")
    odd = lax.rem(me, 2)
    pair = me + 1 - 2 * odd
    far = span // 2
    square = n == 8
    chip = me // 2

    def sends(which, j):
        there = me + 2 * j < n
        return there & (chip != 1) if square and which == DK and j == 1 else there
    score = (score_a, score_b, score_c)

    def load_kv(g, which):
        columns = pl.ds(pl.multiple_of(g * ATT_DIM, ATT_DIM), ATT_DIM)
        source = (keys, values)[which]
        return pltpu.make_async_copy(
            source.at[:, columns], kv.at[g, 0, which], load.at[2 + 2 * g + which]
        )

    def start_load(g, _):
        load_kv(g, 0).start()
        load_kv(g, 1).start()
        return 0

    lax.fori_loop(0, kv_count, start_load, 0)
    load_query = pltpu.make_async_copy(query_hbm, query, load.at[0])
    load_grad = pltpu.make_async_copy(grad_hbm, grad, load.at[1])
    load_query.start()
    load_grad.start()

    def signal(barrier, target):
        pl.semaphore_signal(barrier, inc=1, device_id={"seq": target}, device_id_type=MESH)

    barrier = pltpu.get_barrier_semaphore()
    signal(barrier, pair)
    for j in range(1, far + 1):
        @pl.when(me + 2 * j < n)
        def _():
            signal(barrier, me + 2 * j)

        @pl.when(me - 2 * j >= 0)
        def _():
            signal(barrier, me - 2 * j)

    def clear(g, _):
        for k in range(1, span):
            @pl.when(me - k < 0)
            def _():
                kv[g, k] = jnp.zeros((2, rows, ATT_DIM), BF16)
        return 0

    lax.fori_loop(0, kv_count, clear, 0)
    q_lane = lax.broadcasted_iota(jnp.int32, (1, rows), 1)
    position = q_lane + me * rows
    start = jnp.zeros((1, rows), jnp.int32)
    end = 0
    for i in range(lengths.shape[0]):
        end = end + lengths[i]
        start = jnp.where(position >= end, end, start)

    k_row = lax.broadcasted_iota(jnp.int32, (rows, rows), 0)
    for k in range(span):
        allow = k_row >= start - (me - k) * rows
        if k == 0:
            allow = allow & (k_row <= q_lane)
        bias[k * rows:(k + 1) * rows, :] = jnp.where(allow, 0.0, MASKED)
    value_t[ATT_DIM:, :] = jnp.ones((ONES, value_t.shape[1]), BF16)
    pl.semaphore_wait(
        barrier, 1 + jnp.minimum(me // 2, far) + jnp.minimum((n - 1 - me) // 2, far)
    )

    def remote(source, target, send_sem, recv_sem, device):
        return pltpu.make_async_remote_copy(
            src_ref=source, dst_ref=target, send_sem=send_sem, recv_sem=recv_sem,
            device_id={"seq": device}, device_id_type=MESH,
        )

    def gather(g, which, j):
        return remote(
            kv.at[g, 0, which], kv.at[g, 2 * j, which], gather_send.at[g, which, 2 * j],
            gather_recv.at[g, which, 2 * j], me + 2 * j,
        )

    def hand_on(g, which, j, slot):
        return remote(
            kv.at[g, 2 * j, which], kv.at[g, slot, which], gather_send.at[g, which, slot],
            gather_recv.at[g, which, slot], pair,
        )

    def each_hand_on(first, last, act):
        for j in range(first, last + 1):
            if j >= 1:
                @pl.when((odd == 1) & (me - 2 * j >= 0))
                def _():
                    act(j, 2 * j - 1)
            if j < far:
                @pl.when((odd == 0) & (me - 2 * j >= 0))
                def _():
                    act(j, 2 * j + 1)

    def begin(g):
        for which in (DK, DV):
            for j in range(1, far + 1):
                @pl.when(sends(which, j))
                def _():
                    gather(g, which, j).start()
            each_hand_on(0, 0, lambda j, slot: hand_on(g, which, j, slot).start())

    load_kv(0, DK).wait()
    load_kv(0, DV).wait()
    begin(0)

    def relay(g):
        return remote(
            kv.at[g, 4, DK], kv.at[g, 2, DK], relay_send.at[g],
            gather_recv.at[g, DK, 2], me - 2,
        )

    def relay_keys(g):
        if square:
            @pl.when(chip == 3)
            def _():
                gather(g, DK, 2).wait_recv()
                relay(g).start()

    def pass_on(g, which):
        for j in range(far, 0, -1):
            there = me - 2 * j >= 0
            if square and which == DK and j == 2:
                there = there & (chip != 3)

            @pl.when(there)
            def _():
                gather(g, which, j).wait_recv()
            each_hand_on(j, j, lambda j, slot: hand_on(g, which, j, slot).start())

    def handed(g, which):
        for k in range(1, span, 2):
            @pl.when(me - k >= 0)
            def _():
                hand_on(g, which, 0, k).wait_recv()

    def partial(g, which, k):
        part = acc[g, which, :, k * rows:(k + 1) * rows]
        return part * (1.0 / scale) if which == DV else part

    def to_pair(g, which, k, j):
        return remote(
            sent.at[g, which, k], mix.at[g, which, j], back_send.at[g, which, k],
            mix_recv.at[g, which, j], pair,
        )

    def back(g, which, j):
        return remote(
            sent.at[g, which, 2 * j], got.at[g, which, j], back_send.at[g, which, 2 * j],
            back_recv.at[g, which, j], me - 2 * j,
        )

    def each_to_pair(act):
        for k in range(1, span, 2):
            @pl.when((odd == 1) & (me - k >= 0))
            def _():
                act(k, (k - 1) // 2)

            @pl.when((odd == 0) & (me - k >= 0))
            def _():
                act(k, (k + 1) // 2)

    def share_partial(g, which):
        def act(k, j):
            sent[g, which, k] = partial(g, which, k).astype(BF16)
            to_pair(g, which, k, j).start()

        each_to_pair(act)

    def wait_mix(g, which, j):
        to_pair(g, which, 1, j).wait_recv()

    def combine(g, which):
        for j in range(far, 0, -1):
            def give(mixed):
                part = partial(g, which, 2 * j)
                if mixed:
                    wait_mix(g, which, j)
                    part = part + mix[g, which, j].astype(F32)
                sent[g, which, 2 * j] = part.astype(BF16)
                back(g, which, j).start()

            if j < far:
                @pl.when(me - 2 * j >= 0)
                def _():
                    give(True)
            else:
                @pl.when((me - 2 * j >= 0) & (odd == 1))
                def _():
                    give(True)

                @pl.when((me - 2 * j >= 0) & (odd == 0))
                def _():
                    give(False)

    def at(k):
        return slice(k * rows, (k + 1) * rows)

    for g in range(1, kv_count):
        load_kv(g, DK).wait()
        load_kv(g, DV).wait()
    load_query.wait()
    load_grad.wait()

    def near(i, _):
        for u in range(4):
            h = 4 * i + u
            g = h // share
            columns = pl.ds(pl.multiple_of(h * ATT_DIM, ATT_DIM), ATT_DIM)
            query_t[h] = query[:, columns].T
            cot_t[h] = grad[:, columns].T
            s = lax.dot_general(kv[g, 0, 0], query_t[h], NN, preferred_element_type=F32)
            s = s + bias[at(0), :]
            near_score[h] = s
            most = s[:FOLD]
            for r in range(FOLD, rows, FOLD):
                most = jnp.maximum(most, s[r:r + FOLD])
            near_top[h] = most
            near_slope[h] = lax.dot_general(
                kv[g, 0, 1], cot_t[h], NN, preferred_element_type=F32
            )
        return 0

    lax.fori_loop(0, kv_count * share // 4, near, 0)
    relay_keys(0)
    pass_on(0, DK)
    pass_on(0, DV)

    def group(g, _):
        handed(g, DK)
        handed(g, DV)
        if kv_count > 1:
            @pl.when(g + 1 < kv_count)
            def _():
                begin(g + 1)

        def columns(h):
            return pl.ds(pl.multiple_of((g * share + h) * ATT_DIM, ATT_DIM), ATT_DIM)

        def add(which, h, k, a, b):
            part = lax.dot_general(a, b, NT, preferred_element_type=F32)
            if h:
                part = acc[g, which, :, at(k)] + part
            acc[g, which, :, at(k)] = part

        def scores(h, slot):
            most = near_top[g * share + h]
            for k in range(1, span):
                s = lax.dot_general(
                    kv[g, k, 0], query_t[g * share + h], NN, preferred_element_type=F32
                )
                s = s + bias[at(k), :]
                score[slot][at(k - 1), :] = s
                for r in range(0, rows, FOLD):
                    most = jnp.maximum(most, s[r:r + FOLD])
                yield
            top[slot] = jnp.max(most, axis=0, keepdims=True)

        def softmax(h, slot):
            peak = top[slot]
            out_t = jnp.zeros((ATT_DIM + ONES, rows), F32)
            for k in range(span):
                s = score[slot][at(k - 1), :] if k else near_score[g * share + h]
                p = jnp.exp2((s - peak) * (scale * LOG2E)).astype(BF16)
                prob[h, at(k), :] = p
                out_t = out_t + lax.dot_general(
                    value_t[:, at(k)], p, NN, preferred_element_type=F32
                )
                yield
            inverse = 1.0 / out_t[ATT_DIM:ATT_DIM + 1]
            out_t = out_t[:ATT_DIM] * inverse
            out[:, columns(h)] = out_t.astype(BF16).T
            factor = inverse * scale
            factors[h] = factor
            g_t = cot_t[g * share + h].astype(F32) * factor
            delta[h] = jnp.sum(g_t * out_t, axis=0, keepdims=True)
            grad_t[h] = g_t.astype(BF16)

        def value_sums(h):
            for k in range(span):
                add(DV, h, k, grad_t[h], prob[h, at(k), :])
                yield

        def slopes(h, slot):
            for k in range(1, span):
                score[slot][at(k - 1), :] = lax.dot_general(
                    kv[g, k, 1], grad_t[h], NN, preferred_element_type=F32
                )
                yield

        def key_sums(h, slot):
            low = delta[h]
            dq = jnp.zeros((ATT_DIM, rows), F32)
            for k in range(span):
                if k:
                    dp = score[slot][at(k - 1), :]
                else:
                    dp = near_slope[g * share + h] * factors[h]
                ds = prob[h, at(k), :] * (dp - low).astype(BF16)
                dq = dq + lax.dot_general(key_t[:, at(k)], ds, NN, preferred_element_type=F32)
                add(DK, h, k, query_t[g * share + h], ds)
                yield
            query_grad[:, columns(h)] = dq.astype(BF16).T

        def turn(target, which):
            for k in range(span):
                target[:ATT_DIM, at(k)] = kv[g, k, which].T
                yield

        def ahead(h):
            if h < share:
                return scores(h, h % 3)
            return slopes(h - share, h % 3)

        half = share // 2
        interleave(ahead(0), ahead(1), turn(value_t, 1))
        for h in range(share):
            runs = [softmax(h, h % 3), ahead(h + 2)]
            if h > 1:
                runs.append(value_sums(h - 2))
            if h == share - 2:
                runs.append(turn(key_t, 0))
            interleave(*runs)
        interleave(value_sums(share - 2), value_sums(share - 1))
        share_partial(g, DV)
        store_heads(0, g).start()
        if kv_count > 1:
            @pl.when(g + 1 < kv_count)
            def _():
                relay_keys(g + 1)

            @pl.when(g >= 1)
            def _():
                combine(g - 1, DK)
        for h in range(share):
            if h == half:
                combine(g, DV)
                if kv_count > 1:
                    @pl.when(g + 1 < kv_count)
                    def _():
                        pass_on(g + 1, DK)
                        pass_on(g + 1, DV)
            runs = [key_sums(h, (h + share) % 3)]
            if h + 2 < share:
                runs.append(slopes(h + 2, (h + 2 + share) % 3))
            interleave(*runs)
        store_heads(1, g).start()
        share_partial(g, DK)
        return 0

    def store_heads(which, g):
        wide = share * ATT_DIM
        columns = pl.ds(pl.multiple_of(g * wide, wide), wide)
        source, target = ((out, out_hbm), (query_grad, query_grad_hbm))[which]
        return pltpu.make_async_copy(
            source.at[:, columns], target.at[:, columns], store.at[which, g]
        )

    lax.fori_loop(0, kv_count, group, 0)
    combine(kv_count - 1, DK)
    def finish(g, _):
        columns = pl.ds(pl.multiple_of(g * ATT_DIM, ATT_DIM), ATT_DIM)
        for which, target in ((DV, value_grad), (DK, key_grad)):
            unit = scale if which == DV else 1.0

            @pl.when(odd == 0)
            def _():
                wait_mix(g, which, 0)
                acc[g, which, :, 0:rows] += mix[g, which, 0].astype(F32) * unit

            for j in range(1, far + 1):
                @pl.when(me + 2 * j < n)
                def _():
                    back(g, which, j).wait_recv()
                    acc[g, which, :, 0:rows] += got[g, which, j].astype(F32) * unit
            target[:, columns] = partial(g, which, 0).T.astype(BF16)
            for j in range(1, far + 1):
                @pl.when(me - 2 * j >= 0)
                def _():
                    back(g, which, j).wait_send()
            each_to_pair(lambda k, j: to_pair(g, which, k, j).wait_send())
        for which in (DK, DV):
            for j in range(1, far + 1):
                @pl.when(sends(which, j))
                def _():
                    gather(g, which, j).wait_send()
            each_hand_on(
                0, far, lambda j, slot: hand_on(g, which, j, slot).wait_send()
            )
            store_heads(which, g).wait()
        if square:
            @pl.when(chip == 3)
            def _():
                relay(g).wait_send()
        return 0

    lax.fori_loop(0, kv_count, finish, 0)


def deliver(*refs):
    sources, targets, buffers = refs[:4], refs[4:8], refs[8:12]
    first, second = refs[12], refs[13]
    parts = []
    for i in range(4):
        rows = sources[i].shape[0]
        cuts = 4 if i < 2 else 1
        for c in range(cuts):
            at = pl.ds(c * rows // cuts, rows // cuts)
            m = len(parts)
            parts.append((
                pltpu.make_async_copy(sources[i].at[at], buffers[i].at[at], first.at[m]),
                pltpu.make_async_copy(buffers[i].at[at], targets[i].at[at], second.at[m]),
            ))
    for fetch, _ in parts:
        fetch.start()
    for fetch, write in parts:
        fetch.wait()
        write.start()
    for _, write in parts:
        write.wait()


def on_device(lengths, query, keys, values, attention_grad):
    n = lax.axis_size("seq")
    rows = query.shape[0]
    kv_count = keys.shape[1] // ATT_DIM
    share = query.shape[1] // keys.shape[1]
    span = n // 2 + 1
    whole = pl.BlockSpec(memory_space=pltpu.VMEM)
    hbm = pl.BlockSpec(memory_space=pltpu.HBM)
    keyed = span * rows
    turned = (ATT_DIM, rows)
    results = pl.pallas_call(
        functools.partial(kernel, n, span, kv_count, share),
        out_shape=[
            jax.ShapeDtypeStruct(a.shape, BF16) for a in (query, query, keys, values)
        ],
        in_specs=[pl.BlockSpec(memory_space=pltpu.SMEM)]
        + [pl.BlockSpec(memory_space=pl.ANY)] * 4,
        out_specs=[pl.BlockSpec(memory_space=pl.ANY)] * 2 + [whole] * 2,
        scratch_shapes=[
            pltpu.VMEM(query.shape, BF16),
            pltpu.VMEM(query.shape, BF16),
            pltpu.VMEM(query.shape, BF16),
            pltpu.VMEM(query.shape, BF16),
            pltpu.VMEM((kv_count, span, 2, rows, ATT_DIM), BF16),
            pltpu.VMEM((ATT_DIM, keyed), BF16),
            pltpu.VMEM((ATT_DIM + ONES, keyed), BF16),
            pltpu.VMEM((kv_count * share,) + turned, BF16),
            pltpu.VMEM((kv_count * share,) + turned, BF16),
            pltpu.VMEM((share,) + turned, BF16),
            pltpu.VMEM((share, 1, rows), F32),
            pltpu.VMEM((share, 1, rows), F32),
            pltpu.VMEM((3, 1, rows), F32),
            pltpu.VMEM((kv_count * share, FOLD, rows), F32),
            pltpu.VMEM((kv_count * share, rows, rows), F32),
            pltpu.VMEM((kv_count * share, rows, rows), F32),
            pltpu.VMEM((keyed, rows), F32),
            pltpu.VMEM((keyed, rows), F32),
            pltpu.VMEM((keyed, rows), F32),
            pltpu.VMEM((keyed, rows), F32),
            pltpu.VMEM((share, keyed, rows), BF16),
            pltpu.VMEM((kv_count, 2, ATT_DIM, keyed), F32),
            pltpu.VMEM((kv_count, 2, span) + turned, BF16),
            pltpu.VMEM((kv_count, 2, span // 2 + 1) + turned, BF16),
            pltpu.VMEM((kv_count, 2, span // 2 + 1) + turned, BF16),
            pltpu.SemaphoreType.DMA((2 + 2 * kv_count,)),
            pltpu.SemaphoreType.DMA((2, kv_count)),
            pltpu.SemaphoreType.DMA((kv_count, 2, span)),
            pltpu.SemaphoreType.DMA((kv_count, 2, span)),
            pltpu.SemaphoreType.DMA((kv_count, 2, span)),
            pltpu.SemaphoreType.DMA((kv_count, 2, span // 2 + 1)),
            pltpu.SemaphoreType.DMA((kv_count, 2, span // 2 + 1)),
            pltpu.SemaphoreType.DMA((kv_count,)),
        ],
        compiler_params=pltpu.CompilerParams(
            collective_id=0, has_side_effects=True, vmem_limit_bytes=60 << 20
        ),
    )(lengths, query, keys, values, attention_grad)
    return pl.pallas_call(
        deliver,
        out_shape=[jax.ShapeDtypeStruct(a.shape, BF16) for a in results],
        in_specs=[hbm] * 4,
        out_specs=[hbm] * 4,
        scratch_shapes=[pltpu.VMEM(a.shape, BF16) for a in results]
        + [pltpu.SemaphoreType.DMA((10,)), pltpu.SemaphoreType.DMA((10,))],
    )(*results)


def solution(mesh):
    in_specs = (P(), P("seq", "head"), P("seq", "head"), P("seq", "head"), P("seq", "head"))
    out_specs = (P("seq", "head"), P("seq", "head"), P("seq", "head"), P("seq", "head"))
    return jax.shard_map(
        on_device, mesh=mesh, in_specs=in_specs, out_specs=out_specs, check_vma=False
    )
```
